32 devices in a mesh: ens: 2 (over y), lon: 4 (over z), lat: 4 (over x, core).
Axes of the slice: x: 2, y: 2, z: 4, core: 2. Of those that a mesh axis runs over, the one named last changes fastest.
Arguments:
- field: float32 [8, 1440, 640], P(('ens', 'lat'), 'lon'), parts along dimension 0, may hold values from -6 to 6
- piece_lengths: int32 [4], replicated, may hold values from 1 to 360, 720 in all
- offsets: int32 [4], replicated, may hold values from 0 to 2, as said below
- basis: float32 [9, 4, 2, 17], replicated, may hold values from -1 to 1
- depth_weight: float32 [9, 640], replicated, may hold values from -2 to 2
- gain: float32 [640], replicated, may hold values from 0.5 to 1.5
- w_in: bfloat16 [640, 1280], replicated, may hold values from -0.25 to 0.25
- b_in: float32 [1280], replicated, may hold values from -3 to 3
- w_out: bfloat16 [1280, 640], replicated, may hold values from -0.15625 to 0.15625
- b_out: float32 [640], replicated, may hold values from -3 to 3
Outputs:
- result: float32 [8, 1440, 640], P(('ens', 'lat'), 'lon'), parts along dimension 0
The draws below stay inside these ranges and needn't reach their ends.
There are 2 independent parts, one for each index of `ens`. The reference program is written for one: setup_inputs(seed, part) draws one part's arguments, and reference() takes and returns one part's arrays. A program takes and returns all parts, laid end to end along the dimension named above; an argument that names none is the same for every part. Nothing has to cross between parts.
Inputs may be any that keep to these rules, and one draw needn't show every extreme that they name: Index b of lon holds longitudes starts[b] to starts[b] + piece_lengths[b] - 1 in its first piece_lengths[b] slots; the lengths sum to 720. Output row i reads latitude rows offsets[i] to offsets[i] + 1, and i - 1 <= offsets[i] <= i.
All inputs are finite; a program needn't handle non-finite values.
Results may differ from the reference program's by a relative error of at most 0.0018.
Values sent between devices are 32-bit elements; how exact they have to be, the bound alone decides.
No kernel may reach another device: no remote copies, remote signals or barrier semaphores. Data moves between devices by JAX's collectives and lax.ppermute only.
A program may use at most 64 MiB of HBM per device.

```python
import math
import jax
import jax.numpy as jnp
import numpy as np
from jax import lax

C = 640
HID = 1280
NLON = 720
NB = 9
LW = 17
NLAT = 4
SPAN = 2
LCAP = 360
N_LON = 4


def draw_offsets(key, part):
    rows = jnp.arange(NLAT, dtype=jnp.int32)
    lag = jax.random.randint(jax.random.fold_in(key, 71), (NLAT,), 0, SPAN, dtype=jnp.int32)
    return jnp.clip(rows - lag, 0, NLAT - SPAN).astype(jnp.int32)


def block_scale(stream_key, shape, split, least, top_value):
    loudness, own = 1.0, jax.random.fold_in(stream_key, 6)
    for position, blocks in split:
        heights = jnp.exp(jax.random.uniform(jax.random.fold_in(own, position), (blocks,), jnp.float32, least / len(split), top_value / len(split)))
        loudness = loudness * jnp.repeat(heights, shape[position] // blocks).reshape([-1 if axis == position else 1 for axis in range(len(shape))])
    return loudness


def length_profile(amount, total, limit, slope):
    portions = [(1 << 20) // math.isqrt(grade ** slope) + 1 for grade in range(2, amount + 1)]
    rest, holding = total - limit - (amount - 1), [1] * (amount - 1)
    while rest > 0:
        free = [i for i in range(amount - 1) if holding[i] < limit]
        pool, remaining = sum([portions[i] for i in free]), rest
        for i in free:
            addition = min(limit - holding[i], max(1, remaining * portions[i] // pool), rest)
            holding[i] = holding[i] + addition
            rest = rest - addition
    return np.array([limit] + holding)


def uneven(key, number_of, total, bound, lean):
    if number_of == 2:
        one = jax.random.randint(key, (), max(1, total - bound), min(bound, total - 1) + 1)
        return jnp.stack([one, total - one])
    lengths = jnp.asarray(length_profile(number_of, total, bound, lean), jnp.int32)
    pairs = (number_of - 1) // 2
    donor, sink = lengths[1:1 + 2 * pairs:2], lengths[2:2 + 2 * pairs:2]
    slack = jnp.minimum(donor - 1, bound - sink)
    passed = jax.random.randint(jax.random.fold_in(key, 1), (pairs,), 0, 1 << 20) % (slack + 1)
    lengths = lengths.at[1:1 + 2 * pairs:2].set(donor - passed).at[2:2 + 2 * pairs:2].set(sink + passed)
    return lengths[jax.random.permutation(jax.random.fold_in(key, 2), number_of)]


def normal_values(rng, dims, deviation, bound, split=(), kind=jnp.bfloat16):
    loudness = block_scale(rng, dims, split, -0.22, 0.18) if split else 1.0
    array = jax.random.normal(rng, dims, jnp.float32) * deviation * loudness
    return jnp.minimum(jnp.maximum(array, -bound), bound).astype(kind)


def setup_inputs(seed: int = 0, part: int = 0) -> dict:
    seeds = jax.random.split(jax.random.key(seed), 11)
    part_splits = jax.random.split(jax.random.fold_in(seeds[10], part), 11)
    field = normal_values(part_splits[0], (NLAT, N_LON * LCAP, C), 1.0, 6.0, ((0, 4), (1, 4)), jnp.float32)
    piece_lengths = uneven(seeds[1], N_LON, NLON, LCAP, 2).astype(jnp.int32)
    offsets = draw_offsets(jax.random.fold_in(seeds[10], 71), part)
    basis = normal_values(seeds[3], (NB, NLAT, SPAN, LW), (SPAN * LW) ** -0.5, 1.0, (), jnp.float32)
    depth_weight = normal_values(seeds[4], (NB, C), 0.3333, 2.0, (), jnp.float32)
    gain = jnp.clip(jax.random.uniform(seeds[5], (C,), jnp.float32, 0.5, 1.5), 0.5, 1.5)
    w_in = normal_values(seeds[6], (C, HID), C ** -0.5, 0.25)
    b_in = normal_values(seeds[7], (HID,), 0.5, 3.0, (), jnp.float32)
    w_out = normal_values(seeds[8], (HID, C), HID ** -0.5, 0.15625)
    b_out = normal_values(seeds[9], (C,), 0.5, 3.0, (), jnp.float32)
    return dict(field=field, piece_lengths=piece_lengths, offsets=offsets, basis=basis, depth_weight=depth_weight, gain=gain, w_in=w_in, b_in=b_in, w_out=w_out, b_out=b_out)


def slot_table(piece_lengths):
    starts = (jnp.cumsum(piece_lengths) - piece_lengths).astype(jnp.int32)
    longitudes = jnp.arange(NLON, dtype=jnp.int32)
    owner = (lax.optimization_barrier(jnp.sum((starts[None, :] <= longitudes[:, None]).astype(jnp.int32), axis=1)) - 1).astype(jnp.int32)
    own_start = lax.optimization_barrier(jnp.sum(jnp.where(jnp.arange(N_LON, dtype=jnp.int32)[None, :] == owner[:, None], starts[None, :], 0), axis=1)).astype(jnp.int32)
    return (owner * LCAP + longitudes - own_start).astype(jnp.int32)

def reference(field, piece_lengths, offsets, basis, depth_weight, gain, w_in, b_in, w_out, b_out):
    slot_index = slot_table(piece_lengths)
    dense = jnp.take(field, slot_index, axis=1)
    coefficients = jnp.einsum('kism,kc->ismc', basis, depth_weight, precision=lax.Precision.HIGHEST)
    half_taps = LW // 2

    def one_row(row):
        support = lax.dynamic_slice_in_dim(dense, offsets[row].astype(jnp.int32), SPAN, 0)
        row_coef = coefficients[row]
        total = jnp.zeros((NLON, C), jnp.float32)
        for tap in range(LW):
            shifted = jnp.roll(support, half_taps - tap, axis=1)
            total = total + lax.optimization_barrier(jnp.sum(row_coef[:, tap, :][:, None, :] * shifted, axis=0))
        return total
    conv = lax.map(one_row, jnp.arange(NLAT, dtype=jnp.int32))
    state = dense + conv
    mean_sq = lax.optimization_barrier(jnp.mean(state * state, axis=-1, keepdims=True))
    normed = (state * lax.rsqrt(mean_sq + 1e-05) * gain).astype(jnp.bfloat16).reshape(-1, C)
    pre = jnp.dot(normed, w_in, preferred_element_type=jnp.float32) + b_in
    activated = jax.nn.gelu(pre, approximate=False).astype(jnp.bfloat16)
    mlp_out = jnp.dot(activated, w_out, preferred_element_type=jnp.float32) + b_out
    output = state + mlp_out.reshape(NLAT, NLON, C)
    result = jnp.zeros(field.shape, jnp.float32).at[:, slot_index, :].set(output)
    return result
```

```python
import functools

import jax
import jax.numpy as jnp
from jax import lax
from jax.experimental import pallas as pl
from jax.experimental.pallas import tpu as pltpu
from jax.sharding import PartitionSpec as P

LANES = 128
HBM = pl.BlockSpec(memory_space=pltpu.HBM)
SMEM = pl.BlockSpec(memory_space=pltpu.SMEM)
VMEM = pl.BlockSpec(memory_space=pltpu.VMEM)


def up8(value):
    return (value + 7) // 8 * 8


def in_vmem(value):
    return pltpu.with_memory_space_constraint(value, pltpu.VMEM)


def in_hbm(value):
    return pltpu.with_memory_space_constraint(value, pltpu.HBM)


def grant(mib):
    return pltpu.CompilerParams(vmem_limit_bytes=mib << 20)


def vmem_out(shape, dtype=jnp.float32):
    return pltpu.VMEM(shape, dtype)


def edges_kernel(half, lengths, own, out, rows, sems):
    length = lengths[lax.axis_index("lon")]
    cap = own.shape[0]
    last = jnp.maximum(length - half, 0)
    if cap % 8 == 0:
        base = pl.multiple_of(jnp.minimum(last // 8 * 8, cap - 16), 8)
        head = pltpu.make_async_copy(own.at[pl.ds(0, half), :], out.at[pl.ds(0, half), :], sems.at[0])
        tail = pltpu.make_async_copy(own.at[pl.ds(base, 16), :], rows.at[pl.ds(0, 16), :], sems.at[1])
        head.start()
        tail.start()
        head.wait()
        tail.wait()
        start = last - base
    else:
        whole = pltpu.make_async_copy(own, rows, sems.at[0])
        whole.start()
        whole.wait()
        out[pl.ds(0, half), :] = rows[pl.ds(0, half), :]
        start = last
    for near in range(half):
        out[pl.ds(half + near, 1), :] = rows[pl.ds(start + near, 1), :]


def halo_kernel(count, half, lengths, *refs):
    received, out, stack = refs[:-2], refs[-2], refs[-1]
    me = lax.axis_index("lon")
    for step, ref in enumerate(received):
        stack[pl.ds(step * 2 * half, 2 * half), :] = ref[...]

    def row_of(piece, row):
        behind = lax.rem(me - piece + count, count) - 1
        return behind * (2 * half) + row

    piece = lax.rem(me + count - 1, count)
    slot = lengths[piece] - 1
    for near in range(1, half + 1):
        row = half + slot - jnp.maximum(lengths[piece] - half, 0)
        out[pl.ds(half - near, 1), :] = stack[pl.ds(row_of(piece, row), 1), :]
        before = lax.rem(piece + count - 1, count)
        piece, slot = (
            jnp.where(slot > 0, piece, before),
            jnp.where(slot > 0, slot - 1, lengths[before] - 1),
        )
    piece = lax.rem(me + 1, count)
    slot = jnp.int32(0)
    for near in range(half):
        out[pl.ds(half + near, 1), :] = stack[pl.ds(row_of(piece, slot), 1), :]
        inside = slot + 1 < lengths[piece]
        piece, slot = (
            jnp.where(inside, piece, lax.rem(piece + 1, count)),
            jnp.where(inside, slot + 1, 0),
        )


def fill_window(window, rows, halos, half, length):
    cap = rows.shape[0]
    for column in range(window.shape[0]):
        lanes = pl.ds(column * LANES, LANES)
        window[column, pl.ds(0, half), :] = halos[pl.ds(0, half), lanes]
        window[column, pl.ds(half, cap), :] = rows[:, lanes]
    for column in range(window.shape[0]):
        lanes = pl.ds(column * LANES, LANES)
        window[column, pl.ds(half + length, half), :] = halos[pl.ds(half, half), lanes]


def add_taps(total, window, column, first, rows, coef, taps):
    lanes = pl.ds(column * LANES, LANES)
    for phase in range(min(8, taps)):
        steps = (taps - phase + 7) // 8
        block = window[column, pl.ds(first + phase, rows + 8 * (steps - 1)), :]
        for step in range(steps):
            weight = coef[pl.ds(8 * step + phase, 1), lanes]
            total = total + weight * block[8 * step : 8 * step + rows]
    return total


def own_kernel(half, block, lengths, offsets, basis, depth_weight, own_hbm, halos, *refs):
    held = (len(refs) - 6) // 2
    sources, out, coef_other, copied = refs[:held], refs[held], refs[held + 1], refs[held + 2 : 2 * held + 2]
    window, coef_own, own, sems = refs[2 * held + 2 :]
    own_copy = pltpu.make_async_copy(own_hbm, own, sems.at[0])
    own_copy.start()
    copies = [pltpu.make_async_copy(a, b, sems.at[1]) for a, b in zip(sources, copied)]
    for copy in copies:
        copy.start()
    lat = lax.axis_index("lat")
    length = lengths[lax.axis_index("lon")]
    at = lat - offsets[lat]
    taps = basis.shape[3]
    for which, ref in ((at, coef_own), (1 - at, coef_other)):
        ref[pl.ds(0, taps), :] = lax.dot_general(
            basis[:, lat, which, :],
            depth_weight[...],
            (((0,), (0,)), ((), ())),
            precision=lax.Precision.HIGHEST,
            preferred_element_type=jnp.float32,
        )
    own_copy.wait()
    fill_window(window, own, halos, half, length)
    rows_all = out.shape[0]
    for first in range(0, rows_all, block):
        rows = min(block, rows_all - first)
        for column in range(window.shape[0]):
            state = window[column, pl.ds(half + first, rows), :]
            out[pl.ds(first, rows), pl.ds(column * LANES, LANES)] = add_taps(
                state, window, column, first, rows, coef_own, taps
            )
    for copy in copies:
        copy.wait()


def block_kernel(half, taps, block, lengths, offsets, near, far, near_halo, far_halo, partial, coef, gain,
                 w_in, b_in, w_out, b_out, out, window, state, normed, hidden, result, sem):
    lat = lax.axis_index("lat")
    length = lengths[lax.axis_index("lon")]
    at = lat - offsets[lat]
    use_near = lax.rem(at + lat, 2) == 0
    columns = window.shape[0]
    width = columns * LANES
    cap = near.shape[0]

    @pl.when(use_near)
    def _():
        fill_window(window, near, near_halo, half, length)

    @pl.when(jnp.logical_not(use_near))
    def _():
        fill_window(window, far, far_halo, half, length)

    rows_all = partial.shape[0]
    copies = []
    for first in range(0, rows_all, block):
        rows = min(block, rows_all - first)
        here = pl.ds(first, rows)
        squares = jnp.zeros((rows, LANES), jnp.float32)
        for column in range(columns):
            lanes = pl.ds(column * LANES, LANES)
            value = add_taps(partial[here, lanes], window, column, first, rows, coef, taps)
            squares = squares + value * value
            state[pl.ds(0, rows), lanes] = value
        scale = lax.rsqrt(jnp.sum(squares, axis=1, keepdims=True) / width + 1e-05)
        normed[pl.ds(0, rows), :] = (state[pl.ds(0, rows), :] * scale * gain[...][None, :]).astype(jnp.bfloat16)
        step = 256
        for start in range(0, w_in.shape[1], step):
            part = pl.ds(start, step)
            pre = jnp.dot(normed[pl.ds(0, rows), :], w_in[:, part], preferred_element_type=jnp.float32)
            pre = pre + b_in[part][None, :]
            active = 0.5 * pre * (1.0 + lax.erf(pre * 0.7071067811865476))
            hidden[pl.ds(0, rows), part] = active.astype(jnp.bfloat16)
        inside = (lax.broadcasted_iota(jnp.int32, (rows, 1), 0) + first) < length
        mixed = jnp.dot(hidden[pl.ds(0, rows), :], w_out[...], preferred_element_type=jnp.float32)
        value = jnp.where(inside, state[pl.ds(0, rows), :] + (mixed + b_out[...][None, :]), 0.0)
        if cap % 8:
            kept = min(rows, cap - first)
            result[pl.ds(first, kept), :] = value[:kept]
        else:
            result[here, :] = value
            copy = pltpu.make_async_copy(result.at[here, :], out.at[here, :], sem)
            copy.start()
            copies.append(copy)
    if cap % 8:
        copy = pltpu.make_async_copy(result, out, sem)
        copy.start()
        copies.append(copy)
    for copy in copies:
        copy.wait()


def on_device(field, piece_lengths, offsets, basis, depth_weight, gain, w_in, b_in, w_out, b_out):
    _, cap, channels = field.shape
    count = lax.axis_size("lon")
    lats = lax.axis_size("lat")
    taps = basis.shape[3]
    half = taps // 2
    columns = channels // LANES
    cap8 = up8(cap)
    hid = w_in.shape[1]
    block = 120

    own = in_hbm(field.reshape(cap, channels))
    piece_lengths, offsets = in_hbm(piece_lengths), in_hbm(offsets)
    near_pairs = [(a, a ^ 1) for a in range(lats) if (a ^ 1) < lats]
    far_pairs = [(a, a + 1) for a in range(1, lats - 1, 2)] + [(a + 1, a) for a in range(1, lats - 1, 2)]

    def to_near(value):
        return lax.ppermute(value, "lat", near_pairs)

    def to_far(value):
        return lax.ppermute(value, "lat", far_pairs)

    far = to_far(own)
    near = to_near(own)
    edges = pl.pallas_call(
        functools.partial(edges_kernel, half),
        out_shape=vmem_out((2 * half, channels)),
        in_specs=[SMEM, HBM],
        out_specs=VMEM,
        scratch_shapes=[
            pltpu.VMEM((16 if cap % 8 == 0 else cap, channels), jnp.float32),
            pltpu.SemaphoreType.DMA((2,)),
        ],
        compiler_params=grant(8),
        name="edges",
    )(piece_lengths, own)
    received = [
        lax.ppermute(edges, "lon", [(p, (p + step) % count) for p in range(count)]) for step in range(1, count)
    ]
    halos = pl.pallas_call(
        functools.partial(halo_kernel, count, half),
        out_shape=vmem_out((2 * half, channels)),
        in_specs=[SMEM] + [VMEM] * len(received),
        out_specs=VMEM,
        scratch_shapes=[pltpu.VMEM((max(1, count - 1) * 2 * half, channels), jnp.float32)],
        compiler_params=grant(8),
        name="halo",
    )(piece_lengths, *[in_vmem(r) for r in received])
    near_halo, far_halo = to_near(halos), to_far(halos)
    window = pltpu.VMEM((columns, cap8 + 2 * half + 16, LANES), jnp.float32)
    operands = (gain, w_in, b_in, w_out, b_out)
    partial, coef, *operands = pl.pallas_call(
        functools.partial(own_kernel, half, block),
        out_shape=(
            vmem_out((cap8, channels)),
            vmem_out((up8(taps), channels)),
            *[vmem_out(value.shape, value.dtype) for value in operands],
        ),
        in_specs=[SMEM, SMEM, VMEM, VMEM, HBM, VMEM] + [HBM] * len(operands),
        out_specs=(VMEM,) * (2 + len(operands)),
        scratch_shapes=[
            window,
            pltpu.VMEM((up8(taps), channels), jnp.float32),
            pltpu.VMEM((cap, channels), jnp.float32),
            pltpu.SemaphoreType.DMA((2,)),
        ],
        compiler_params=grant(16),
        name="own",
    )(piece_lengths, offsets, in_hbm(basis), in_hbm(depth_weight), own, halos, *[in_hbm(v) for v in operands])
    most = min(block, cap8)
    out = pl.pallas_call(
        functools.partial(block_kernel, half, taps, block),
        out_shape=jax.ShapeDtypeStruct((cap, channels), jnp.float32),
        in_specs=[SMEM, SMEM] + [VMEM] * 11,
        out_specs=HBM,
        scratch_shapes=[
            window,
            pltpu.VMEM((most, channels), jnp.float32),
            pltpu.VMEM((most, channels), jnp.bfloat16),
            pltpu.VMEM((most, hid), jnp.bfloat16),
            pltpu.VMEM((cap, channels), jnp.float32),
            pltpu.SemaphoreType.DMA,
        ],
        compiler_params=grant(24),
        name="block",
    )(piece_lengths, offsets, in_vmem(near), in_vmem(far), in_vmem(near_halo), in_vmem(far_halo), partial, coef,
      *operands)
    return out.reshape(1, cap, channels)


def solution(mesh):
    placed = (P(("ens", "lat"), "lon", None), P(), P(), P(), P(), P(), P(), P(), P(), P())
    return jax.shard_map(
        on_device,
        mesh=mesh,
        in_specs=placed,
        out_specs=P(("ens", "lat"), "lon", None),
        check_vma=False,
    )
```

```python
import functools

import jax
import jax.numpy as jnp
from jax import lax
from jax.experimental import pallas as pl
from jax.experimental.pallas import tpu as pltpu
from jax.sharding import PartitionSpec as P

LANES = 128
META = 8
HBM = pl.BlockSpec(memory_space=pltpu.HBM)
SMEM = pl.BlockSpec(memory_space=pltpu.SMEM)
VMEM = pl.BlockSpec(memory_space=pltpu.VMEM)


def up8(value):
    return (value + 7) // 8 * 8


def in_vmem(value):
    return pltpu.with_memory_space_constraint(value, pltpu.VMEM)


def in_hbm(value):
    return pltpu.with_memory_space_constraint(value, pltpu.HBM)


def grant(mib):
    return pltpu.CompilerParams(vmem_limit_bytes=mib << 20)


def vmem_out(shape, dtype=jnp.float32):
    return pltpu.VMEM(shape, dtype)


def load_kernel(count, half, lengths, offsets, own, edges, window, meta, rows, sem):
    me, lat = lax.axis_index("lon"), lax.axis_index("lat")
    columns, cap = window.shape[0], own.shape[0]
    length = lengths[me]
    at = lat - offsets[lat]
    if cap % 8 == 0:
        copies = [
            pltpu.make_async_copy(
                own.at[:, pl.ds(column * LANES, LANES)], window.at[column, pl.ds(half, cap), :], sem
            )
            for column in range(columns)
        ]
    else:
        copies = [pltpu.make_async_copy(own, rows, sem)]
    for copy in copies:
        copy.start()
    meta[0], meta[1], meta[2] = length, at, 1 - lax.rem(at + lat, 2)
    halo_rows(count, half, me, lengths, meta)
    for copy in copies:
        copy.wait()
    zeros = jnp.zeros((half, LANES), jnp.float32)
    last = jnp.maximum(length - half, 0)
    for column in range(columns):
        lanes = pl.ds(column * LANES, LANES)
        if cap % 8:
            window[column, pl.ds(half, cap), :] = rows[:, lanes]
        window[column, pl.ds(0, half), :] = zeros
        edges[pl.ds(0, half), lanes] = window[column, pl.ds(half, half), :]
        edges[pl.ds(half, half), lanes] = window[column, pl.ds(half + last, half), :]
    for column in range(columns):
        window[column, pl.ds(half + length, half), :] = zeros


def halo_rows(count, half, me, lengths, meta):
    def row_of(piece, row):
        return (lax.rem(me - piece + count, count) - 1) * (2 * half) + row

    piece = lax.rem(me + count - 1, count)
    slot = lengths[piece] - 1
    for near in range(1, half + 1):
        meta[META + half - near] = row_of(piece, half + slot - jnp.maximum(lengths[piece] - half, 0))
        before = lax.rem(piece + count - 1, count)
        piece, slot = (
            jnp.where(slot > 0, piece, before),
            jnp.where(slot > 0, slot - 1, lengths[before] - 1),
        )
    piece = lax.rem(me + 1, count)
    slot = jnp.int32(0)
    for near in range(half):
        meta[META + half + near] = row_of(piece, slot)
        inside = slot + 1 < lengths[piece]
        piece, slot = (
            jnp.where(inside, piece, lax.rem(piece + 1, count)),
            jnp.where(inside, slot + 1, 0),
        )


def halo_kernel(half, meta, *refs):
    received, out, stack = refs[:-2], refs[-2], refs[-1]
    for step, ref in enumerate(received):
        stack[pl.ds(step * 2 * half, 2 * half), :] = ref[...]
    for row in range(2 * half):
        out[pl.ds(row, 1), :] = stack[pl.ds(meta[META + row], 1), :]


def fill_window(window, rows, halos, half, length):
    cap = rows.shape[0]
    for column in range(window.shape[0]):
        lanes = pl.ds(column * LANES, LANES)
        window[column, pl.ds(0, half), :] = halos[pl.ds(0, half), lanes]
        window[column, pl.ds(half, cap), :] = rows[:, lanes]
    for column in range(window.shape[0]):
        lanes = pl.ds(column * LANES, LANES)
        window[column, pl.ds(half + length, half), :] = halos[pl.ds(half, half), lanes]


def add_own_halos(partial, halos, coef, edge, half, length, taps):
    columns = partial.shape[0]
    zeros = jnp.zeros((half, LANES), jnp.float32)
    for side, (at, to) in enumerate(((0, half), (2 * half, length))):
        for column in range(columns):
            for part in range(3):
                edge[side, column, pl.ds(part * half, half), :] = zeros
            edge[side, column, pl.ds(at, half), :] = halos[pl.ds(side * half, half), pl.ds(column * LANES, LANES)]
        for column in range(columns):
            here = pl.ds(to, half)
            partial[column, here, :] = add_taps(
                partial[column, here, :], edge.at[side], column, 0, half, coef, taps
            )


def add_taps(total, window, column, first, rows, coef, taps):
    lanes = pl.ds(column * LANES, LANES)
    for phase in range(min(8, taps)):
        steps = (taps - phase + 7) // 8
        block = window[column, pl.ds(first + phase, rows + 8 * (steps - 1)), :]
        for step in range(steps):
            weight = coef[pl.ds(8 * step + phase, 1), lanes]
            total = total + weight * block[8 * step : 8 * step + rows]
    return total


def own_rows(half, block, lower, upper, window, coef, taps, out):
    for first in range(lower, upper, block):
        rows = min(block, upper - first)
        for column in range(window.shape[0]):
            state = window[column, pl.ds(half + first, rows), :]
            out[column, pl.ds(half + first, rows), :] = add_taps(state, window, column, first, rows, coef, taps)


def own_kernel(half, block, split, meta, basis, depth_weight, window, *refs):
    lat = lax.axis_index("lat")
    held = (len(refs) - 4) // 2
    sources, out, coef_own, coef_other = refs[:held], *refs[held : held + 3]
    copied, sem = refs[held + 3 : 2 * held + 3], refs[2 * held + 3]
    copies = [pltpu.make_async_copy(a, b, sem) for a, b in zip(sources, copied)]
    for copy in copies:
        copy.start()
    at = meta[1]
    taps = basis.shape[3]
    for which, ref in ((at, coef_own), (1 - at, coef_other)):
        ref[pl.ds(0, taps), :] = lax.dot_general(
            basis[:, lat, which, :],
            depth_weight[...],
            (((0,), (0,)), ((), ())),
            precision=lax.Precision.HIGHEST,
            preferred_element_type=jnp.float32,
        )
    own_rows(half, block, 0, split, window, coef_own, taps, out)
    for copy in copies:
        copy.wait()


def rest_kernel(half, taps, block, split, upper, meta, window, coef_own, halos, _, out, edge):
    own_rows(half, block, split, upper, window, coef_own, taps, out)
    add_own_halos(out, halos, coef_own, edge, half, meta[0], taps)


def block_kernel(half, taps, block, meta, near, far, near_halo, far_halo, partial, coef, gain,
                 w_in, b_in, w_out, b_out, out, window, state, normed, hidden, result, sem):
    length = meta[0]
    columns = window.shape[0]
    width = columns * LANES
    cap = near.shape[0]
    rows_all = state.shape[0]

    @pl.when(meta[2] == 1)
    def _():
        fill_window(window, near, near_halo, half, length)

    @pl.when(meta[2] == 0)
    def _():
        fill_window(window, far, far_halo, half, length)

    for first in range(0, rows_all, block):
        rows = min(block, rows_all - first)
        here = pl.ds(first, rows)
        for column in range(columns):
            state[here, pl.ds(column * LANES, LANES)] = add_taps(
                partial[column, pl.ds(half + first, rows), :], window, column, first, rows, coef, taps
            )
    for first in range(0, rows_all, 72):
        rows = min(72, rows_all - first)
        here = pl.ds(first, rows)
        value = state[here, :]
        scale = lax.rsqrt(jnp.sum(value * value, axis=1, keepdims=True) / width + 1e-05)
        normed[here, :] = (value * scale * gain[...][None, :]).astype(jnp.bfloat16)
    step = 256
    for start in range(0, w_in.shape[1], step):
        part = pl.ds(start, step)
        pre = jnp.dot(normed[...], w_in[:, part], preferred_element_type=jnp.float32)
        pre = pre + b_in[part][None, :]
        active = 0.5 * pre * (1.0 + lax.erf(pre * 0.7071067811865476))
        hidden[:, part] = active.astype(jnp.bfloat16)
    inside = lax.broadcasted_iota(jnp.int32, (rows_all, 1), 0) < length
    copies = []
    for start in range(0, width, step):
        part = pl.ds(start, min(step, width - start))
        mixed = jnp.dot(hidden[...], w_out[:, part], preferred_element_type=jnp.float32)
        value = jnp.where(inside, state[:, part] + (mixed + b_out[part][None, :]), 0.0)
        result[:, part] = value[:cap]
        copy = pltpu.make_async_copy(result.at[:, part], out.at[:, part], sem)
        copy.start()
        copies.append(copy)
    for copy in copies:
        copy.wait()


def on_device(field, piece_lengths, offsets, basis, depth_weight, gain, w_in, b_in, w_out, b_out):
    _, cap, channels = field.shape
    count = lax.axis_size("lon")
    lats = lax.axis_size("lat")
    taps = basis.shape[3]
    half = taps // 2
    columns = channels // LANES
    cap8 = up8(cap)
    hid = w_in.shape[1]
    block = 120

    own = in_hbm(field.reshape(cap, channels))
    piece_lengths, offsets = in_hbm(piece_lengths), in_hbm(offsets)
    near_pairs = [(a, a ^ 1) for a in range(lats) if (a ^ 1) < lats]
    far_pairs = [(a, a + 1) for a in range(1, lats - 1, 2)] + [(a + 1, a) for a in range(1, lats - 1, 2)]

    def to_near(value):
        return lax.ppermute(value, "lat", near_pairs)

    parts = lax.axis_size("ens")
    far_full = [(e * lats + a, e * lats + b) for e in range(parts) for a, b in far_pairs]
    far_full += [(e * lats + a, (e + 1) % parts * lats + a) for e in range(parts) for a in (0, lats - 1)]

    def to_far(value):
        return lax.ppermute(value, ("ens", "lat"), far_full)

    far = to_far(own)
    near = to_near(own)
    padded = (columns, cap8 + 2 * half + 16, LANES)
    edges, window, meta = pl.pallas_call(
        functools.partial(load_kernel, count, half),
        out_shape=(
            vmem_out((2 * half, channels)),
            vmem_out(padded),
            pltpu.SMEM((META + 2 * half,), jnp.int32),
        ),
        in_specs=[SMEM, SMEM, HBM],
        out_specs=(VMEM, VMEM, SMEM),
        scratch_shapes=[
            pltpu.VMEM((8 if cap % 8 == 0 else cap, channels), jnp.float32),
            pltpu.SemaphoreType.DMA,
        ],
        compiler_params=grant(8),
        name="load",
    )(piece_lengths, offsets, own)
    received = [
        lax.ppermute(edges, "lon", [(p, (p + step) % count) for p in range(count)]) for step in range(1, count)
    ]
    operands = (gain, w_in, b_in, w_out, b_out)
    split = min(120, cap8)
    partial, coef_own, coef, *operands = pl.pallas_call(
        functools.partial(own_kernel, half, block, split),
        out_shape=(
            vmem_out(padded),
            vmem_out((up8(taps), channels)),
            vmem_out((up8(taps), channels)),
            *[vmem_out(value.shape, value.dtype) for value in operands],
        ),
        in_specs=[SMEM, VMEM, VMEM, VMEM] + [HBM] * len(operands),
        out_specs=(VMEM,) * (3 + len(operands)),
        scratch_shapes=[pltpu.SemaphoreType.DMA],
        compiler_params=grant(8),
        name="own",
    )(meta, in_hbm(basis), in_hbm(depth_weight), window, *[in_hbm(v) for v in operands])
    partial, *held = lax.optimization_barrier((partial, *received))
    halos = pl.pallas_call(
        functools.partial(halo_kernel, half),
        out_shape=vmem_out((2 * half, channels)),
        in_specs=[SMEM] + [VMEM] * len(held),
        out_specs=VMEM,
        scratch_shapes=[pltpu.VMEM((max(1, count - 1) * 2 * half, channels), jnp.float32)],
        compiler_params=grant(8),
        name="halo",
    )(meta, *[in_vmem(r) for r in held])
    near_halo, far_halo = to_near(halos), to_far(halos)
    partial = pl.pallas_call(
        functools.partial(rest_kernel, half, taps, block, split, cap8),
        out_shape=vmem_out(padded),
        in_specs=[SMEM, VMEM, VMEM, VMEM, VMEM],
        out_specs=VMEM,
        scratch_shapes=[pltpu.VMEM((2, columns, 3 * half, LANES), jnp.float32)],
        input_output_aliases={4: 0},
        compiler_params=grant(8),
        name="rest",
    )(meta, window, coef_own, halos, partial)
    out = pl.pallas_call(
        functools.partial(block_kernel, half, taps, block),
        out_shape=jax.ShapeDtypeStruct((cap, channels), jnp.float32),
        in_specs=[SMEM] + [VMEM] * 11,
        out_specs=HBM,
        scratch_shapes=[
            pltpu.VMEM(padded, jnp.float32),
            pltpu.VMEM((cap8, channels), jnp.float32),
            pltpu.VMEM((cap8, channels), jnp.bfloat16),
            pltpu.VMEM((cap8, hid), jnp.bfloat16),
            pltpu.VMEM((cap, channels), jnp.float32),
            pltpu.SemaphoreType.DMA,
        ],
        compiler_params=grant(24),
        name="block",
    )(meta, in_vmem(near), in_vmem(far), in_vmem(near_halo), in_vmem(far_halo), partial, coef, *operands)
    return out.reshape(1, cap, channels)


def solution(mesh):
    placed = (P(("ens", "lat"), "lon", None), P(), P(), P(), P(), P(), P(), P(), P(), P())
    return jax.shard_map(
        on_device,
        mesh=mesh,
        in_specs=placed,
        out_specs=P(("ens", "lat"), "lon", None),
        check_vma=False,
    )
```
